32 devices in a mesh: gx: 8 (over z, core), gy: 4 (over y, x).
Axes of the slice: x: 2, y: 2, z: 4, core: 2. Of those that a mesh axis runs over, the one named last changes fastest.
Arguments:
- mesh_state: bfloat16 [128, 128, 32, 128], P('gx', 'gy'), may hold values from -6 to 6
- part_feat: bfloat16 [131072, 128], P(('gx', 'gy')), may hold values from -6 to 6
- cell_index: int32 [131072], P(('gx', 'gy')), may hold values from 0 to 16383, as said below
- pairs: int32 [2, 786432], P(None, ('gx', 'gy')), may hold values from 0 to 4095, as said below
- dest: int32 [131072], P(('gx', 'gy')), may hold values from 0 to 8, as said below
- mass: float32 [131072], P(('gx', 'gy')), may hold values from 0.5 to 2
- velocity: float32 [3, 131072], P(None, ('gx', 'gy')), may hold values from -30 to 30
- w_enc: bfloat16 [128, 128], replicated, may hold values from -0.5 to 0.5
- w_mesh: bfloat16 [128, 128], replicated, may hold values from -0.21875 to 0.21875
- w_pair: bfloat16 [128, 256], replicated, may hold values from -0.5 to 0.5
- w_edge: bfloat16 [128, 128], replicated, may hold values from -0.5 to 0.5
- w_node: bfloat16 [256, 128], replicated, may hold values from -0.25 to 0.25
- w_accel: bfloat16 [3, 128], replicated, may hold values from -0.5 to 0.5
Outputs:
- mesh_out: bfloat16 [128, 128, 32, 128], P('gx', 'gy')
- stay_feat: bfloat16 [131072, 128], P(('gx', 'gy'))
- stay_vel: float32 [3, 131072], P(None, ('gx', 'gy'))
- arrived_feat: bfloat16 [32768, 128], P(('gx', 'gy'))
- arrived_vel: float32 [4, 32768], P(None, ('gx', 'gy'))
The draws below stay inside these ranges and needn't reach their ends.
Inputs may be any that keep to these rules, and one draw needn't show every extreme that they name: `dest`: 0 means the particle stays; k from 1 to 8 moves it in the k-th direction of the steps. At most 128 particles of one device take any one direction, and some device receives 128 particles from each of its eight neighbours. `cell_index`: A device's particles come in 8 aligned groups of 512 rows; the particles of group g lie in cells g * 2048 to (g + 1) * 2048 - 1 of the device's block. `pairs`: A device's columns come in 8 aligned groups of 3072; both rows of a column of group g name particles of the device's group g, rows g * 512 to (g + 1) * 512 - 1.
All inputs are finite; a program needn't handle non-finite values.
Results may differ from the reference program's by a relative error of at most 0.0085.
Values may be sent and summed in bfloat16 or wider, within the bound.
A program may use at most 128 MiB of HBM per device.

```python
import math
import jax
import jax.numpy as jnp
from jax import lax

F = 128
C = 128
CX = 16
CY = 32
CZ = 32
PART_DEV = 4096
NBR = 6
GRP = 512
NGRP = 8
EDGE_DEV = 24576
CELLS_DEV = 16384
NX = 128
NY = 128
PARTICLES = 131072
EDGES = 786432
N_GX = 8
N_GY = 4
DEVICES = 32


def draw_cell_index(key, part):
    span = CELLS_DEV // NGRP
    row = jnp.arange(PARTICLES, dtype=jnp.int32) % PART_DEV
    group = row // GRP
    local = jax.random.randint(jax.random.fold_in(key, 31), (PARTICLES,), 0, span)
    return (local + group * span).astype(jnp.int32)


def draw_pairs(key, part):
    column = jnp.arange(EDGES, dtype=jnp.int32) % EDGE_DEV
    group = column // (GRP * NBR)
    local = jax.random.randint(jax.random.fold_in(key, 37), (2, EDGES), 0, GRP)
    return (local + group[None, :] * GRP).astype(jnp.int32)


def draw_dest(key, part):
    keys = jax.random.split(jax.random.fold_in(key, 11), 4)
    level = jax.random.randint(keys[0], (DEVICES,), 0, 5)
    rate = 16 * jnp.left_shift(jnp.ones((DEVICES,), jnp.int32), level.astype(jnp.int32))
    target = jax.random.randint(keys[1], (), 0, DEVICES)
    target_x = target // N_GY
    target_y = target % N_GY
    device = jnp.arange(DEVICES, dtype=jnp.int32)
    rel_x = (device // N_GY - target_x + N_GX) % N_GX
    rel_y = (device % N_GY - target_y + N_GY) % N_GY
    near_x = (rel_x <= 1) | (rel_x == N_GX - 1)
    near_y = (rel_y <= 1) | (rel_y == N_GY - 1)
    forced = near_x & near_y
    pick = jax.random.randint(keys[2], (DEVICES, PART_DEV), 0, 1024)
    way = jax.random.randint(keys[3], (DEVICES, PART_DEV), 1, 9)
    cyclic = jnp.arange(PART_DEV, dtype=jnp.int32) % 8 + 1
    chosen = jnp.where(pick < rate[:, None], way, 0)
    chosen = jnp.where(forced[:, None], cyclic[None, :], chosen)
    onehot = (chosen[:, :, None] == jnp.arange(1, 9, dtype=jnp.int32)[None, None, :]).astype(jnp.int32)
    place = jnp.sum(jnp.cumsum(onehot, axis=1) * onehot, axis=2)
    capacity = PART_DEV // 32
    chosen = jnp.where(place > capacity, 0, chosen)
    return chosen.reshape(-1).astype(jnp.int32)


def draw_velocity(key, part):
    keys = jax.random.split(jax.random.fold_in(key, 23), 2)
    device = jnp.arange(PARTICLES, dtype=jnp.int32) // PART_DEV
    ramp = 1.0 + 2.0 * device.astype(jnp.float32) / max(DEVICES - 1, 1)
    common = jax.random.uniform(keys[0], (3, 1), jnp.float32, 0.5, 1.5)
    noise = jnp.clip(jax.random.normal(keys[1], (3, PARTICLES), jnp.float32), -6.0, 6.0)
    return ((noise + common) * ramp[None, :]).astype(jnp.float32)


def steps_of(rng, extent, pieces, smallest, largest):
    loudness, own = 1.0, jax.random.fold_in(rng, 6)
    for axis_at, shards_of in pieces:
        draws = jnp.exp(jax.random.uniform(jax.random.fold_in(own, axis_at), (shards_of,), jnp.float32, smallest / len(pieces), largest / len(pieces)))
        loudness = loudness * jnp.repeat(draws, extent[axis_at] // shards_of).reshape([-1 if axis == axis_at else 1 for axis in range(len(extent))])
    return loudness


def centred(stream_key, dims, scale, reach, shards=(), kind=jnp.bfloat16):
    entries = jax.random.normal(stream_key, dims, jnp.float32) * scale
    if len(shards) > 0:
        entries = steps_of(stream_key, dims, shards, -0.22, 0.18) * entries
    return jnp.clip(entries, min=-reach, max=reach).astype(kind)


def setup_inputs(seed: int = 0) -> dict:
    key_list = jax.random.split(jax.random.key(seed), 14)
    mesh_state = centred(key_list[0], (NX, NY, CZ, C), 1.0, 6.0, ((0, 8), (1, 4)))
    part_feat = centred(key_list[1], (PARTICLES, F), 1.0, 6.0, ((0, 32),))
    cell_index = draw_cell_index(jax.random.fold_in(key_list[13], 71), 0)
    pairs = draw_pairs(jax.random.fold_in(key_list[13], 71), 0)
    dest = draw_dest(jax.random.fold_in(key_list[13], 71), 0)
    mass = jnp.clip(jnp.exp(math.log(2.0) - 1.3862944 * jax.random.uniform(key_list[5], (PARTICLES,), jnp.float32) ** steps_of(key_list[5], (PARTICLES,), ((0, 32),), -0.2, 0.2)), 0.5, 2.0)
    velocity = draw_velocity(jax.random.fold_in(key_list[13], 71), 0)
    w_enc = centred(key_list[7], (F, C), F ** -0.5, 0.5)
    w_mesh = centred(key_list[8], (C, C), (6 * C) ** -0.5, 0.21875)
    w_pair = centred(key_list[9], (F, 2 * F), F ** -0.5, 0.5)
    w_edge = centred(key_list[10], (F, F), F ** -0.5, 0.5)
    w_node = centred(key_list[11], (F + C, F), (4 * F) ** -0.5, 0.25)
    w_accel = centred(key_list[12], (3, F), F ** -0.5, 0.5)
    return {"mesh_state": mesh_state, "part_feat": part_feat, "cell_index": cell_index, "pairs": pairs, "dest": dest, "mass": mass, "velocity": velocity, "w_enc": w_enc, "w_mesh": w_mesh, "w_pair": w_pair, "w_edge": w_edge, "w_node": w_node, "w_accel": w_accel}


directions = ((-1, -1), (-1, 0), (-1, 1), (0, -1), (0, 1), (1, -1), (1, 0), (1, 1))


def encode(state_rows, feat, cell, w_enc):
    deposit = jnp.zeros((state_rows.shape[0], feat.shape[1]), jnp.float32).at[cell].add(feat.astype(jnp.float32))
    deposit = deposit.astype(jnp.bfloat16)
    return (state_rows.astype(jnp.float32) + jnp.dot(deposit, w_enc, preferred_element_type=jnp.float32)).astype(jnp.bfloat16)


def zsides(field):
    padded = jnp.pad(field, [(0, 0)] * (field.ndim - 2) + [(1, 1), (0, 0)])
    return padded[..., 2:, :] + padded[..., :-2, :]


def mesh_update(centre, sides, w_mesh):
    width = centre.shape[-1]
    summed = sides.astype(jnp.bfloat16).reshape(-1, width)
    update = jnp.dot(summed, w_mesh, preferred_element_type=jnp.float32).reshape(centre.shape)
    return (centre.astype(jnp.float32) + jax.nn.silu(update)).astype(jnp.bfloat16)


def particle_step(feat, cell, pair, mesh_rows, w_pair, w_edge, w_node):
    width = feat.shape[1]
    proj = jnp.dot(feat, w_pair, preferred_element_type=jnp.float32).astype(jnp.bfloat16)
    proj_send = proj[:, :width]
    proj_recv = proj[:, width:]
    count = pair.shape[1]
    block = min(12288, count)
    turns = count // block
    senders = pair[0].reshape(turns, block)
    receivers = pair[1].reshape(turns, block)

    def edge_block(total, index):
        pre = proj_send[index[0]].astype(jnp.float32) + proj_recv[index[1]].astype(jnp.float32)
        act = jax.nn.silu(pre).astype(jnp.bfloat16)
        message = jnp.dot(act, w_edge, preferred_element_type=jnp.float32)
        return total.at[index[1]].add(message), None

    start = jnp.zeros((feat.shape[0], width), jnp.float32)
    edge_sum, _ = lax.scan(edge_block, start, (senders, receivers))
    edge_sum = edge_sum.astype(jnp.bfloat16)
    near = mesh_rows[cell]
    update = jnp.dot(edge_sum, w_node[:width], preferred_element_type=jnp.float32)
    update = update + jnp.dot(near, w_node[width:], preferred_element_type=jnp.float32)
    return (feat.astype(jnp.float32) + jax.nn.silu(update)).astype(jnp.bfloat16)


def readout(h_new, w_accel):
    return lax.dot_general(w_accel, h_new, (((1,), (1,)), ((), ())), preferred_element_type=jnp.float32)


def pack(h_new, vel1, mass, dest, cap):
    ways = jnp.arange(1, 9, dtype=jnp.int32)
    onehot = (dest[:, None] == ways[None, :]).astype(jnp.int32)
    slot = jnp.sum((jnp.cumsum(onehot, axis=0) - 1) * onehot, axis=1).astype(jnp.int32)
    group = jnp.where(dest > 0, dest - 1, 8).astype(jnp.int32)
    feats = jnp.zeros((8, cap, h_new.shape[1]), jnp.bfloat16).at[group, slot].set(h_new, mode="drop")
    extra = jnp.concatenate([vel1, mass[None, :]], axis=0).T.astype(jnp.bfloat16)
    moving = jnp.zeros((8, cap, 4), jnp.bfloat16).at[group, slot].set(extra, mode="drop")
    return feats, jnp.transpose(moving, (0, 2, 1))


def unpack(moving, drift):
    values = moving.astype(jnp.float32)
    weight = values[..., 3:4, :]
    speed = jnp.where(weight > 0, values[..., :3, :] - drift[:, None], 0.0)
    return jnp.concatenate([speed, weight], axis=-2)


def to_blocks(whole):
    width = whole.shape[-1]
    grid = whole.reshape(N_GX, CX, N_GY, CY, CZ, width).transpose(0, 2, 1, 3, 4, 5)
    return grid.reshape(N_GX * N_GY, CX * CY * CZ, width)


def from_blocks(blocks):
    width = blocks.shape[-1]
    grid = blocks.reshape(N_GX, N_GY, CX, CY, CZ, width).transpose(0, 2, 1, 3, 4, 5)
    return grid.reshape(CX * N_GX, CY * N_GY, CZ, width)


def stencil(mesh1, w_mesh):
    planes = mesh1.shape[0]

    def one_plane(xpos):
        below = lax.dynamic_index_in_dim(mesh1, (xpos + planes - 1) % planes, 0, keepdims=False).astype(jnp.float32)
        above = lax.dynamic_index_in_dim(mesh1, (xpos + 1) % planes, 0, keepdims=False).astype(jnp.float32)
        centre_raw = lax.dynamic_index_in_dim(mesh1, xpos, 0, keepdims=False)
        centre = centre_raw.astype(jnp.float32)
        sides = below + above + jnp.roll(centre, 1, axis=0) + jnp.roll(centre, -1, axis=0) + zsides(centre)
        return mesh_update(centre_raw, sides, w_mesh)

    return lax.map(one_plane, jnp.arange(planes, dtype=jnp.int32))


def reference(mesh_state, part_feat, cell_index, pairs, dest, mass, velocity, w_enc, w_mesh, w_pair, w_edge, w_node, w_accel):
    devices = N_GX * N_GY
    width = part_feat.shape[1]
    feat_b = part_feat.reshape(devices, PART_DEV, width)
    cell_b = cell_index.reshape(devices, PART_DEV)
    pairs_b = pairs.reshape(2, devices, EDGE_DEV).transpose(1, 0, 2)
    dest_b = dest.reshape(devices, PART_DEV)
    mass_b = mass.reshape(devices, PART_DEV)
    vel_b = velocity.reshape(3, devices, PART_DEV).transpose(1, 0, 2)
    state_b = to_blocks(mesh_state)
    mesh1_b = lax.map(lambda item: encode(item[0], item[1], item[2], w_enc), (state_b, feat_b, cell_b))
    mesh2 = stencil(from_blocks(mesh1_b), w_mesh)
    mesh2_b = to_blocks(mesh2)

    def one_device(item):
        feat, cell, pair, rows, speed = item
        h_new = particle_step(feat, cell, pair, rows, w_pair, w_edge, w_node)
        return h_new, speed + readout(h_new, w_accel)

    h_b, vel1_b = lax.map(one_device, (feat_b, cell_b, pairs_b, mesh2_b, vel_b))
    momentum = jnp.sum(mass_b[:, None, :] * vel1_b, axis=(0, 2))
    drift = momentum / jnp.sum(mass)
    staying = dest_b == 0
    stay_feat = jnp.where(staying[:, :, None], h_b, jnp.zeros_like(h_b)).reshape(-1, width)
    stay_vel = jnp.where(staying[:, None, :], vel1_b - drift[None, :, None], 0.0)
    stay_vel = stay_vel.transpose(1, 0, 2).reshape(3, -1)
    cap = PART_DEV // 32
    feats_b, moving_b = lax.map(lambda item: pack(item[0], item[1], item[2], item[3], cap), (h_b, vel1_b, mass_b, dest_b))
    feats_g = feats_b.reshape(N_GX, N_GY, 8, cap, width)
    moving_g = moving_b.reshape(N_GX, N_GY, 8, 4, cap)
    got_f = []
    got_m = []
    for index, offset in enumerate(directions):
        got_f.append(jnp.roll(feats_g[:, :, index], offset, axis=(0, 1)))
        got_m.append(jnp.roll(moving_g[:, :, index], offset, axis=(0, 1)))
    arrived_feat = jnp.stack(got_f, axis=2).reshape(-1, width)
    arrived = unpack(jnp.stack(got_m, axis=2), drift)
    arrived_vel = arrived.transpose(3, 0, 1, 2, 4).reshape(4, -1)
    return mesh2, stay_feat, stay_vel, arrived_feat, arrived_vel
```

```python
import functools
import jax
import jax.numpy as jnp
from jax import lax
from jax.experimental import pallas as pl
from jax.experimental.pallas import tpu as pltpu
from jax.sharding import PartitionSpec as P

directions = ((-1, -1), (-1, 0), (-1, 1), (0, -1), (0, 1), (1, -1), (1, 0), (1, 1))
LANES = 128
VMEM_LIMIT = 60 * 1024 * 1024


def from_behind(block, axis, distance):
    devices = range(lax.axis_size(axis))
    route = [((i - distance) % len(devices), i) for i in devices]
    return lax.ppermute(block, axis, route)


def summed_over(total, axis):
    devices = lax.axis_size(axis)
    if devices & (devices - 1):
        return lax.psum(total, axis)
    distance = 1
    while distance < devices:
        total = total + from_behind(total, axis, distance)
        distance *= 2
    return total


def group_sizes(parts, cells):
    members = min(512, parts)
    count = parts // members
    return (members, count, cells // count)


def silu(v):
    half = 0.5 * v
    return half + half * jnp.tanh(half)


def f32dot(a, b):
    return jnp.dot(a, b, preferred_element_type=jnp.float32)


def row_hot(keys, rows, first):
    lanes = lax.broadcasted_iota(jnp.int32, (rows, keys.shape[1]), 0) + first
    return jnp.where(lanes == keys, 1.0, 0.0).astype(jnp.bfloat16)


def col_hot(cols, start, stop, width):
    lanes = lax.broadcasted_iota(jnp.int32, (LANES, width), 1)
    parts = [
        jnp.where(lanes == cols[:, j : j + 1], 1.0, 0.0).astype(jnp.bfloat16)
        for j in range(start, stop)
    ]
    return jnp.concatenate(parts, axis=0)


def encode_kernel(chunk, cell_ref, feat_ref, state_ref, w_enc_ref, out_ref):
    span = state_ref.shape[0]
    base = pl.program_id(0) * span
    cells = cell_ref[0] - base

    def body(i, carry):
        first = pl.multiple_of(i * chunk, chunk)
        onehot = row_hot(cells, chunk, first)
        deposit = f32dot(onehot, feat_ref[...]).astype(jnp.bfloat16)
        rows = pl.ds(first, chunk)
        out_ref[rows, :] = (
            state_ref[rows, :].astype(jnp.float32) + f32dot(deposit, w_enc_ref[...])
        ).astype(jnp.bfloat16)
        return carry

    lax.fori_loop(0, span // chunk, body, 0)


def edge_kernel(
    members, send_ref, recv_ref, recv_row_ref, feat_ref, w_pair_ref, w_edge_ref, out_ref
):
    base = pl.program_id(0) * members
    width = feat_ref.shape[1]
    proj = f32dot(feat_ref[...], w_pair_ref[...]).astype(jnp.bfloat16)
    table = jnp.concatenate([proj[:, :width], proj[:, width:]], axis=0)
    send_cols = (send_ref[0] - base).T
    recv_cols = (recv_ref[0] - base).T
    turns = send_cols.shape[1]
    step = 6 if turns % 6 == 0 else 1
    total = jnp.zeros((members, width), jnp.float32)
    for start in range(0, turns, step):
        hot = jnp.concatenate(
            [
                col_hot(send_cols, start, start + step, members),
                col_hot(recv_cols, start, start + step, members),
            ],
            axis=1,
        )
        act = silu(f32dot(hot, table)).astype(jnp.bfloat16)
        keys = recv_row_ref[0, :, start * LANES : (start + step) * LANES] - base
        total = total + f32dot(row_hot(keys, members, 0), act)
    edge_sum = f32dot(total.astype(jnp.bfloat16), w_edge_ref[...])
    out_ref[...] = edge_sum.astype(jnp.bfloat16)


def node_kernel(
    plane,
    depth,
    cap,
    below_ref,
    centre_ref,
    above_ref,
    xlo_ref,
    xhi_ref,
    ylo_ref,
    yhi_ref,
    cell_ref,
    dest_ref,
    dest_row_ref,
    edge_ref,
    feat_ref,
    mass_ref,
    vel_ref,
    w_mesh_ref,
    w_node_ref,
    w_accel_ref,
    mesh_ref,
    stay_ref,
    vel1_ref,
    packed_ref,
    total_ref,
    slots_ref,
    carry_ref,
):
    step = pl.program_id(0)
    last = pl.num_programs(0) - 1
    span, width = centre_ref.shape
    members = feat_ref.shape[0]
    planes = span // plane
    base = step * span

    @pl.when(step == 0)
    def _():
        slots_ref[...] = jnp.zeros_like(slots_ref)
        carry_ref[...] = jnp.zeros_like(carry_ref)
        total_ref[...] = jnp.zeros_like(total_ref)

    level = lax.broadcasted_iota(jnp.int32, (plane, width), 0) % depth
    for p in range(planes):
        rows = slice(p * plane, (p + 1) * plane)
        centre = centre_ref[rows, :].astype(jnp.float32)
        if p == 0:
            below = jnp.where(
                step == 0, xlo_ref[...].astype(jnp.float32), below_ref[...].astype(jnp.float32)
            )
        else:
            below = centre_ref[(p - 1) * plane : p * plane, :].astype(jnp.float32)
        if p == planes - 1:
            above = jnp.where(
                step == last, xhi_ref[...].astype(jnp.float32), above_ref[...].astype(jnp.float32)
            )
        else:
            above = centre_ref[(p + 1) * plane : (p + 2) * plane, :].astype(jnp.float32)
        edge = slice(p * depth, (p + 1) * depth)
        left = jnp.concatenate([ylo_ref[edge, :].astype(jnp.float32), centre[:-depth]], axis=0)
        right = jnp.concatenate([centre[depth:], yhi_ref[edge, :].astype(jnp.float32)], axis=0)
        down = jnp.where(level == 0, 0.0, pltpu.roll(centre, 1, 0))
        up = jnp.where(level == depth - 1, 0.0, pltpu.roll(centre, plane - 1, 0))
        sides = (below + above + left + right + (up + down)).astype(jnp.bfloat16)
        mesh_ref[rows, :] = (centre + silu(f32dot(sides, w_mesh_ref[...]))).astype(jnp.bfloat16)

    cell_cols = (cell_ref[0] - base).T
    dest_cols = dest_ref[0].T
    turns = members // LANES
    near = f32dot(col_hot(cell_cols, 0, turns, span), mesh_ref[...]).astype(jnp.bfloat16)
    update = f32dot(edge_ref[...], w_node_ref[:width, :]) + f32dot(near, w_node_ref[width:, :])
    h_new = (feat_ref[...].astype(jnp.float32) + silu(update)).astype(jnp.bfloat16)
    h_wide = h_new.astype(jnp.float32)
    for j in range(turns):
        rows = slice(j * LANES, (j + 1) * LANES)
        stay_ref[rows, :] = jnp.where(dest_cols[:, j : j + 1] == 0, h_wide[rows], 0.0).astype(
            jnp.bfloat16
        )
    accel = lax.dot_general(
        w_accel_ref[...], h_new, (((1,), (1,)), ((), ())), preferred_element_type=jnp.float32
    )
    vel1 = vel_ref[...] + accel[:3]
    mass = mass_ref[0]
    vel1_ref[...] = vel1
    sums = jnp.concatenate([mass * vel1, mass], axis=0)
    total_ref[...] += sum(sums[:, j * LANES : (j + 1) * LANES] for j in range(turns))

    dest = dest_row_ref[0]
    ways = lax.broadcasted_iota(jnp.int32, (8, members), 0) + 1
    chosen_way = jnp.where(ways == dest, 1.0, 0.0)
    earlier = jnp.where(
        lax.broadcasted_iota(jnp.int32, (members, members), 0)
        < lax.broadcasted_iota(jnp.int32, (members, members), 1),
        1.0,
        0.0,
    ).astype(jnp.bfloat16)
    place = f32dot(chosen_way.astype(jnp.bfloat16), earlier) + carry_ref[:, :1]
    slot = jnp.sum(place * chosen_way, axis=0, keepdims=True).astype(jnp.int32)
    carry_ref[...] += jnp.sum(chosen_way, axis=1, keepdims=True)
    key = jnp.where(dest > 0, (dest - 1) * cap + slot, -1)
    extra = jnp.concatenate([vel1, mass, jnp.zeros((LANES - 4, members), jnp.float32)], axis=0)
    values = jnp.concatenate([h_new, extra.T.astype(jnp.bfloat16)], axis=1)
    half = slots_ref.shape[0] // 2
    for first in (0, half):
        rows = slice(first, first + half)
        slots_ref[rows, :] += f32dot(row_hot(key, half, first), values)

    @pl.when(step == last)
    def _():
        moving = slots_ref[:, width:].T
        for k in range(8):
            rows = slice(k * cap, (k + 1) * cap)
            packed_ref[k, :cap, :] = slots_ref[rows, :width].astype(jnp.bfloat16)
            packed_ref[k, cap:, :] = moving[:16, rows].astype(jnp.bfloat16)


def unpack(moving, drift):
    values = moving.astype(jnp.float32)
    weight = values[..., 3:4, :]
    speed = jnp.where(weight > 0, values[..., :3, :] - drift[:, None], 0.0)
    return jnp.concatenate([speed, weight], axis=-2)


def whole(shape):
    return pl.BlockSpec(shape, lambda g: (0,) * len(shape))


def shards(
    mesh_state,
    part_feat,
    cell_index,
    pairs,
    dest,
    mass,
    velocity,
    w_enc,
    w_mesh,
    w_pair,
    w_edge,
    w_node,
    w_accel,
):
    shape = mesh_state.shape
    parts, width = part_feat.shape
    cx, cy, cz, channels = shape
    cells = cx * cy * cz
    plane = cy * cz
    members, count, span = group_sizes(parts, cells)
    planes = span // plane
    per_group = pairs.shape[1] // count
    cap = parts // 32
    bf16, f32 = (jnp.bfloat16, jnp.float32)
    params = pltpu.CompilerParams(vmem_limit_bytes=VMEM_LIMIT)

    by_rows = pl.BlockSpec((members, width), lambda g: (g, 0))
    by_cells = pl.BlockSpec((span, channels), lambda g: (g, 0))
    by_row = pl.BlockSpec((1, 1, members), lambda g: (g, 0, 0))
    by_tile = pl.BlockSpec((1, members // LANES, LANES), lambda g: (g, 0, 0))

    cell_row = cell_index.reshape(count, 1, members)
    cell_tile = cell_index.reshape(count, members // LANES, LANES)
    dest_row = dest.reshape(count, 1, members)
    dest_tile = dest.reshape(count, members // LANES, LANES)
    mass_row = mass.reshape(count, 1, members)
    send_tile = pairs[0].reshape(count, per_group // LANES, LANES)
    recv_tile = pairs[1].reshape(count, per_group // LANES, LANES)
    recv_row = pairs[1].reshape(count, 1, per_group)
    accel8 = jnp.pad(w_accel, ((0, 8 - w_accel.shape[0]), (0, 0)))

    mesh1 = pl.pallas_call(
        functools.partial(encode_kernel, min(512, span)),
        grid=(count,),
        out_shape=jax.ShapeDtypeStruct((cells, channels), bf16),
        in_specs=[by_row, by_rows, by_cells, whole(w_enc.shape)],
        out_specs=by_cells,
        compiler_params=params,
        cost_estimate=pl.CostEstimate(
            flops=2 * cells * members * width, bytes_accessed=4 * cells * channels, transcendentals=0
        ),
        name="encode",
    )(cell_row, part_feat, mesh_state.reshape(cells, channels), w_enc)

    grid1 = mesh1.reshape(shape)
    xlo = from_behind(grid1[cx - 1 :].reshape(plane, channels), "gx", 1)
    xhi = from_behind(grid1[:1].reshape(plane, channels), "gx", -1)
    ylo = from_behind(grid1[:, cy - 1 :].reshape(cx * cz, channels), "gy", 1)
    yhi = from_behind(grid1[:, :1].reshape(cx * cz, channels), "gy", -1)

    by_pairs = pl.BlockSpec((1, per_group // LANES, LANES), lambda g: (g, 0, 0))
    edge_sum = pl.pallas_call(
        functools.partial(edge_kernel, members),
        grid=(count,),
        out_shape=jax.ShapeDtypeStruct((parts, width), bf16),
        in_specs=[
            by_pairs,
            by_pairs,
            pl.BlockSpec((1, 1, per_group), lambda g: (g, 0, 0)),
            by_rows,
            whole(w_pair.shape),
            whole(w_edge.shape),
        ],
        out_specs=by_rows,
        compiler_params=params,
        cost_estimate=pl.CostEstimate(
            flops=6 * pairs.shape[1] * members * width,
            bytes_accessed=4 * parts * width,
            transcendentals=pairs.shape[1] * width,
        ),
        name="edges",
    )(send_tile, recv_tile, recv_row, part_feat, w_pair, w_edge)

    one_plane = lambda f: pl.BlockSpec((plane, channels), f)
    by_layer = pl.BlockSpec((planes * cz, channels), lambda g: (g, 0))
    by_speed = pl.BlockSpec((3, members), lambda g: (0, g))
    mesh2, stay_feat, vel1, packed, totals = pl.pallas_call(
        functools.partial(node_kernel, plane, cz, cap),
        grid=(count,),
        out_shape=(
            jax.ShapeDtypeStruct((cells, channels), bf16),
            jax.ShapeDtypeStruct((parts, width), bf16),
            jax.ShapeDtypeStruct((3, parts), f32),
            jax.ShapeDtypeStruct((8, cap + 16, width), bf16),
            jax.ShapeDtypeStruct((4, LANES), f32),
        ),
        in_specs=[
            one_plane(lambda g: (jnp.maximum(g * planes - 1, 0), 0)),
            by_cells,
            one_plane(lambda g: (jnp.minimum(g * planes + planes, cx - 1), 0)),
            whole((plane, channels)),
            whole((plane, channels)),
            by_layer,
            by_layer,
            by_tile,
            by_tile,
            by_row,
            by_rows,
            by_rows,
            by_row,
            by_speed,
            whole(w_mesh.shape),
            whole(w_node.shape),
            whole(accel8.shape),
        ],
        out_specs=(
            by_cells,
            by_rows,
            by_speed,
            whole((8, cap + 16, width)),
            whole((4, LANES)),
        ),
        scratch_shapes=[
            pltpu.VMEM((8 * cap, width + LANES), f32),
            pltpu.VMEM((8, LANES), f32),
        ],
        compiler_params=params,
        name="nodes",
    )(
        mesh1,
        mesh1,
        mesh1,
        xlo,
        xhi,
        ylo,
        yhi,
        cell_tile,
        dest_tile,
        dest_row,
        edge_sum,
        part_feat,
        mass_row,
        velocity,
        w_mesh,
        w_node,
        accel8,
    )

    sums = jnp.sum(summed_over(summed_over(totals, "gx"), "gy"), axis=1)
    drift = sums[:3] / sums[3]
    stay_vel = jnp.where((dest == 0)[None, :], vel1 - drift[:, None], 0.0)

    got = [packed[k] for k in range(8)]
    for axis, part in (("gx", 0), ("gy", 1)):
        for distance in (1, -1):
            chosen = [k for k, offset in enumerate(directions) if offset[part] == distance]
            moved = from_behind(jnp.stack([got[k] for k in chosen], axis=0), axis, distance)
            for place, k in enumerate(chosen):
                got[k] = moved[place]
    arrived = jnp.stack(got, axis=0)
    arrived_feat = arrived[:, :cap].reshape(-1, width)
    arrived_vel = unpack(arrived[:, cap : cap + 4], drift).transpose(1, 0, 2).reshape(4, -1)
    return (mesh2.reshape(shape), stay_feat, stay_vel, arrived_feat, arrived_vel)


def solution(mesh):
    placed = (
        P("gx", "gy", None, None),
        P(("gx", "gy"), None),
        P(("gx", "gy")),
        P(None, ("gx", "gy")),
        P(("gx", "gy")),
        P(("gx", "gy")),
        P(None, ("gx", "gy")),
        P(),
        P(),
        P(),
        P(),
        P(),
        P(),
    )
    return jax.shard_map(
        shards,
        mesh=mesh,
        in_specs=placed,
        out_specs=(
            P("gx", "gy", None, None),
            P(("gx", "gy"), None),
            P(None, ("gx", "gy")),
            P(("gx", "gy"), None),
            P(None, ("gx", "gy")),
        ),
        check_vma=False,
    )
```
